512 devices in a mesh: dp: 16 (over z, core), expert: 32 (over y, x).
Axes of the slice: x: 4, y: 8, z: 8, core: 2. Of those that a mesh axis runs over, the one named last changes fastest.
Arguments:
- tokens: bfloat16 [2048, 4096], P(('dp', 'expert')), may hold values from -6 to 6
- expert_ids: int32 [2048, 8], P(('dp', 'expert')), may hold values from 0 to 31, all different within a row; in each aligned block of 4 rows (0 to 3, 4 to 7, ...) at most 2 rows name the same one
- gate_probs: float32 [2048, 8], P(('dp', 'expert')), may hold values from 0.2 to 1
- w_gate: bfloat16 [32, 4096, 2048], P('expert', None, 'dp'), may hold values from -0.09375 to 0.09375
- w_up: bfloat16 [32, 4096, 2048], P('expert', None, 'dp'), may hold values from -0.09375 to 0.09375
- w_down: bfloat16 [32, 2048, 4096], P('expert', None, 'dp'), may hold values from -0.125 to 0.125
Outputs:
- combined: bfloat16 [2048, 4096], P(('dp', 'expert'))
The draws below stay inside these ranges and needn't reach their ends.
Inputs may be any that keep to these rules, and one draw needn't show every extreme that they name: `expert_ids`: each row names 8 different experts. In the rows of one device (aligned blocks of 4 rows) no expert is named by more than 2 rows, a bound that some block reaches.
All inputs are finite; a program needn't handle non-finite values.
Results may differ from the reference program's by a relative error of at most 0.0057.
Values may be sent and summed in bfloat16 or wider, within the bound.
A program may use at most 64 MiB of HBM per device.

```python
import math
import jax
import jax.numpy as jnp
import numpy as np
from jax import lax

D = 4096
HID = 2048
TOP = 8
TOK_DEV = 4
EXPERTS = 32
TOKENS = 2048
CAP = 2
SLOTS = 1024


def block_scale(rng, extent, cuts, smallest, high):
    loudness = 1.0
    for dim, shards_of in cuts:
        steps = jax.random.uniform(jax.random.fold_in(jax.random.fold_in(rng, 6), dim), (shards_of,), jnp.float32, smallest / len(cuts), high / len(cuts))
        loudness = loudness * jnp.repeat(jnp.exp(steps), extent[dim] // shards_of).reshape((-1,) + (1,) * (len(extent) - 1 - dim))
    return loudness


def shared_out(stream_key, own, number, rows, count, top, limit, skew):
    ranking = jax.random.permutation(stream_key, count)
    heavy_load, ordinary = portions_of(count, rows * top, limit, skew, True), portions_of(count, rows * top, limit, skew, False)
    places = jnp.arange(count)

    def named(sizes, offset_by):
        used = int((sizes > 0).sum())
        fixed = max(1, used // 4)
        passed = fixed + (places - fixed + offset_by * (used - fixed)) % max(1, count - fixed)
        return jnp.zeros((count,), jnp.int32).at[ranking[jnp.where(places < fixed, places, passed)]].set(jnp.asarray(sizes, jnp.int32))

    sizes = jnp.where(number % 4 == 0, named(heavy_load, number // 4), named(ordinary, number - number // 4 - 1))
    mixed = jax.random.permutation(jax.random.fold_in(own, 3), count)
    source_of, taker = mixed[0:count // 2 * 2:2], mixed[1:count // 2 * 2:2]
    room = jnp.minimum(sizes[source_of] - 1, limit - sizes[taker]) // 2
    room = jnp.where((source_of == ranking[0]) | (taker == ranking[0]) | (sizes[taker] == 0), 0, jnp.maximum(room, 0))
    passed = jax.random.randint(jax.random.fold_in(own, 4), (count // 2,), 0, 1 << 20) % (room + 1)
    sizes = sizes.at[source_of].add(-passed).at[taker].add(passed)
    members = jnp.searchsorted(jnp.cumsum(sizes), jnp.arange(rows * top), side="right").astype(jnp.int32)
    grid = members.reshape(top, rows).T
    grid = grid[jax.random.permutation(jax.random.fold_in(own, 1), rows)]
    offset_by = jax.random.randint(jax.random.fold_in(own, 2), (rows, 1), 0, top)
    return jnp.take_along_axis(grid, (jnp.arange(top)[None, :] + offset_by) % top, axis=1)


def portions_of(amount, total, most, slope, full):
    weights = [(1 << 20) // math.isqrt(grade ** slope) + 1 for grade in range(1, amount + 1)]
    largest = most if full else min(most, max(-(-total // amount), total * weights[0] // sum(weights)))
    least = 1 if total - largest >= amount - 1 else 0
    holding, surplus = [largest] + [least] * (amount - 1), total - largest - least * (amount - 1)
    while surplus > 0:
        free = [i for i in range(1, amount) if holding[i] < largest] or [i for i in range(1, amount) if holding[i] < most]
        mass, remaining = sum([weights[i] for i in free]), surplus
        for i in free:
            more = min(most - holding[i], max(1, remaining * weights[i] // mass), surplus)
            holding[i] = holding[i] + more
            surplus = surplus - more
    return np.array(holding)


def scatter_about(key, extent, deviation, most, shards=(), kind=jnp.bfloat16):
    drawn = jax.random.normal(key, extent, jnp.float32) * deviation
    if len(shards) > 0:
        drawn = block_scale(key, extent, shards, -0.22, 0.18) * drawn
    return jnp.clip(drawn, min=-most, max=most).astype(kind)


def setup_inputs(seed: int = 0) -> dict:
    streams_of = jax.random.split(jax.random.key(seed), 7)
    tokens = scatter_about(streams_of[0], (TOKENS, D), 1.0, 6.0, ((0, 512),))
    expert_ids_keys = jax.random.split(jax.random.fold_in(streams_of[1], 1), TOKENS // TOK_DEV)
    expert_ids_turns = jax.random.permutation(jax.random.fold_in(streams_of[1], 3), TOKENS // TOK_DEV)
    expert_ids = jax.vmap(lambda own, number: shared_out(jax.random.fold_in(streams_of[1], 2), own, number, TOK_DEV, EXPERTS, TOP, CAP, 2))(expert_ids_keys, expert_ids_turns).reshape((TOKENS, TOP))
    gate_probs = jnp.clip(0.2 + 0.8 * jax.random.uniform(streams_of[2], (TOKENS, TOP), jnp.float32) ** block_scale(streams_of[2], (TOKENS, TOP), ((0, 512),), -0.2, 0.2), 0.2, 1.0)
    w_gate = scatter_about(streams_of[3], (EXPERTS, D, HID), D ** -0.5, 0.09375, ((0, 32), (2, 16)))
    w_up = scatter_about(streams_of[4], (EXPERTS, D, HID), D ** -0.5, 0.09375, ((0, 32), (2, 16)))
    w_down = scatter_about(streams_of[5], (EXPERTS, HID, D), HID ** -0.5, 0.125, ((0, 32), (2, 16)))
    return {"tokens": tokens, "expert_ids": expert_ids, "gate_probs": gate_probs, "w_gate": w_gate, "w_up": w_up, "w_down": w_down}


def expand_rows(gathered, gate_matrix, up_matrix):
    gate_proj = jnp.dot(gathered, gate_matrix, preferred_element_type=jnp.float32)
    up_proj = jnp.dot(gathered, up_matrix, preferred_element_type=jnp.float32)
    return (jax.nn.silu(gate_proj) * up_proj).astype(jnp.bfloat16)


def reference(tokens, expert_ids, gate_probs, w_gate, w_up, w_down):
    flat_ids = expert_ids.reshape(-1).astype(jnp.int32)
    flat_gates = gate_probs.reshape(-1)
    owners = (jnp.arange(flat_ids.shape[0], dtype=jnp.int32) // TOP).astype(jnp.int32)

    def one_expert(expert_index, running):
        matches = flat_ids == expert_index
        picked = jnp.nonzero(matches, size=SLOTS, fill_value=0)[0].astype(jnp.int32)
        present = jnp.arange(SLOTS, dtype=jnp.int32) < jnp.sum(matches.astype(jnp.int32))
        targets = owners[picked]
        gathered = tokens[targets]
        hidden = expand_rows(gathered, w_gate[expert_index], w_up[expert_index])
        result = jnp.dot(hidden, w_down[expert_index], preferred_element_type=jnp.float32).astype(jnp.bfloat16)
        result = lax.optimization_barrier(result).astype(flat_gates.dtype)
        scales = jnp.where(present, flat_gates[picked], jnp.zeros((), flat_gates.dtype))
        return running.at[targets].add(result * scales[:, None])

    combined = lax.fori_loop(0, EXPERTS, one_expert, jnp.zeros((TOKENS, D), jnp.float32))
    return combined.astype(jnp.bfloat16)
```

```python
import jax
import jax.numpy as jnp
from jax import lax
from jax.experimental import pallas as pl
from jax.experimental.pallas import tpu as pltpu
from jax.sharding import PartitionSpec as P

MESH = pl.DeviceIdType.MESH
NX, NY, NZ = 4, 8, 8
NE = NX * NY
F32, BF16 = jnp.float32, jnp.bfloat16


def iota(shape, dim):
    return lax.broadcasted_iota(jnp.int32, shape, dim)


def kernel(
    tok_in, meta_in, wg, wu, wd, out,
    tok, metaz, wgu, wdn, xs, hid, outb, rbuf, wrow, fin, final,
    lsem, wssem, wrsem, zssem, zrsem, mssem, mrsem, ssem, rsem,
    hssem, hrsem, ossem, orsem, fssem, frsem,
):
    dp = lax.axis_index("dp")
    ex = lax.axis_index("expert")
    z, core = dp // 2, dp % 2
    y, x = ex // NX, ex % NX
    first = core == 0

    local = [
        pltpu.make_async_copy(wg.at[0], wgu.at[core, :, pl.ds(0, 128)], lsem.at[0]),
        pltpu.make_async_copy(wu.at[0], wgu.at[core, :, pl.ds(128, 128)], lsem.at[1]),
        pltpu.make_async_copy(wd.at[0], wdn.at[core], lsem.at[2]),
        pltpu.make_async_copy(tok_in, tok.at[ex, pl.ds(z * 8, 8)], lsem.at[3]),
        pltpu.make_async_copy(meta_in, metaz.at[z], lsem.at[4]),
    ]
    for copy in local:
        copy.start()

    barrier = pltpu.get_barrier_semaphore()

    def greet(step, carry):
        peer = lax.rem(ex + step, NE)
        pl.semaphore_signal(barrier, inc=1, device_id=(dp, peer), device_id_type=MESH)
        return carry

    lax.fori_loop(1, NE, greet, 0)
    for step in range(1, NZ):
        peer = lax.rem(z + step, NZ) * 2 + core
        pl.semaphore_signal(barrier, inc=1, device_id=(peer, ex), device_id_type=MESH)
    pl.semaphore_signal(barrier, inc=1, device_id=(z * 2 + 1 - core, ex), device_id_type=MESH)
    pl.semaphore_wait(barrier, NE - 1 + NZ - 1 + 1)

    def z_copy(step):
        peer = lax.rem(z + step, NZ)
        return (
            pltpu.make_async_remote_copy(
                meta_in, metaz.at[z], mssem.at[step], mrsem.at[z],
                device_id=(peer * 2 + core, ex), device_id_type=MESH),
            pltpu.make_async_remote_copy(
                tok_in, tok.at[ex, pl.ds(z * 8, 8)], zssem.at[step], zrsem.at[z],
                device_id=(peer * 2 + core, ex), device_id_type=MESH),
        )

    for step in (4, 3, 5, 2, 6, 1, 7):
        for copy in z_copy(step):
            copy.start()

    sibling = (z * 2 + 1 - core, ex)
    weights = [
        pltpu.make_async_remote_copy(
            wg.at[0], wgu.at[core, :, pl.ds(0, 128)], wssem.at[0], wrsem.at[0],
            device_id=sibling, device_id_type=MESH),
        pltpu.make_async_remote_copy(
            wu.at[0], wgu.at[core, :, pl.ds(128, 128)], wssem.at[1], wrsem.at[1],
            device_id=sibling, device_id_type=MESH),
        pltpu.make_async_remote_copy(
            wd.at[0], wdn.at[core], wssem.at[2], wrsem.at[2],
            device_id=sibling, device_id_type=MESH),
    ]
    for copy in weights:
        copy.start()

    local[3].wait()
    local[4].wait()
    for step in range(1, NZ):
        src = lax.rem(z + step, NZ)
        pltpu.make_async_remote_copy(
            meta_in, metaz.at[src], mssem.at[step], mrsem.at[src],
            device_id=sibling, device_id_type=MESH).wait_recv()
    codes = metaz[:, 0, :]
    tok[ex, 64] = jnp.concatenate([codes, jnp.zeros_like(codes)], axis=0).astype(BF16)
    for step in range(1, NZ):
        src = lax.rem(z + step, NZ)
        pltpu.make_async_remote_copy(
            tok_in, tok.at[ex, pl.ds(src * 8, 8)], zssem.at[step], zrsem.at[src],
            device_id=sibling, device_id_type=MESH).wait_recv()

    def place(n, p):
        m = n - 1
        k = m // 2 + 1
        h = m % 2
        i0 = jnp.where(n == 0, p, jnp.where(n == 7, p, 2 * h + p // 2))
        dx0 = jnp.where(i0 == 0, 0, jnp.where(i0 == 1, -1, i0 - 1))
        dy0 = jnp.where(n == 0, 0, jnp.where(n == 7, -4, -k if p % 2 == 0 else k))
        own = (n == 0) | (n == 2)
        opp = n >= 6
        mm = jnp.where(n == 1, 0, n - 2)
        j = jnp.where(own, 2 * n + p, jnp.where(opp, (n - 6) * 4 + p, 2 * mm + p // 2))
        half = (j + 1) // 2
        dy1 = jnp.where(j % 2 == 1, -half, half)
        dx1 = jnp.where(own, 0, jnp.where(opp, 2, -1 if p % 2 == 0 else 1))
        dx = jnp.where(first, dx0, dx1)
        dy = jnp.where(first, dy0, dy1)
        sx = lax.rem(x + dx + NX, NX)
        sy = lax.rem(y + dy + NY, NY)
        mid = (n >= 1) & (n <= 6)
        upto = (k <= 2) | ((k == 3) & (h == (0 if p % 2 == 0 else 1)))
        row = n == 0
        xp0 = row & (p <= 1)
        xm0 = row & (p == 0)
        yp0 = row | (mid & upto & (p % 2 == 0))
        ym0 = row | (mid & upto & (p % 2 == 1))
        side = ~own & ~opp
        xp1 = own | (side & (p == 0))
        xm1 = own | (side & (p == 3))
        yp1 = own & ((j == 0) | ((j % 2 == 1) & (j <= 5)))
        ym1 = own & ((j == 0) | ((j % 2 == 0) & (j >= 2) & (j <= 4)))

        def pick(a, b):
            return (first & a) | (~first & b)

        sends = (pick(xp0, xp1), pick(xm0, xm1), pick(yp0, yp1), pick(ym0, ym1))
        return sy, sx, sends

    right, left = lax.rem(x + 1, NX), lax.rem(x + NX - 1, NX)
    below, above = lax.rem(y + 1, NY), lax.rem(y + NY - 1, NY)
    targets = ((dp, y * NX + right), (dp, y * NX + left), (dp, below * NX + x), (dp, above * NX + x))

    def block_copy(way, idx):
        return pltpu.make_async_remote_copy(
            tok.at[idx], tok.at[idx], ssem.at[way, idx], rsem.at[idx],
            device_id=targets[way], device_id_type=MESH)

    def start_sends(n, p):
        sy, sx, sends = place(n, p)
        idx = sy * NX + sx
        for way in range(4):
            @pl.when(sends[way])
            def _():
                block_copy(way, idx).start()

    def hid_copy(n, step):
        peer = lax.rem(z + step, NZ)
        return pltpu.make_async_remote_copy(
            hid.at[n, z], hid.at[n, z], hssem.at[n, step], hrsem.at[n, z],
            device_id=(peer * 2 + core, ex), device_id_type=MESH)

    def out_copy(n, p):
        sy, sx, _ = place(n, p)
        return pltpu.make_async_remote_copy(
            outb.at[n, p], rbuf.at[ex], ossem.at[n, p], orsem.at[ex],
            device_id=(dp, sy * NX + sx), device_id_type=MESH)

    for way in range(4):
        block_copy(way, ex).start() if way in (2, 3) else None
    for way in (0, 1):
        block_copy(way, ex).start()

    lane = iota((8, 512), 1)
    sub = iota((8, 512), 0)
    depth = iota((128, 512), 0)
    wide = iota((128, 512), 1)
    probs = metaz[:, 1, :]
    hi = probs.astype(BF16)
    rest = probs - hi.astype(F32)
    mid_part = rest.astype(BF16)
    low = (rest - mid_part.astype(F32)).astype(BF16)
    stack = jnp.concatenate([codes.astype(BF16), hi, mid_part, low], axis=0)
    for t in range(4):
        spread = jnp.where(depth == t * 32 + (wide >> 4), 1.0, 0.0).astype(BF16)
        got = jnp.dot(stack, spread, preferred_element_type=F32)
        code = got[0:8]
        prob = got[8:16] + got[16:24] + got[24:32]
        keep = (((lane >> 1) & 7) == sub) & (code == ((lane & 1) + 1).astype(F32))
        wrow[t * 8:(t + 1) * 8, :] = jnp.where(keep, prob, 0.0)

    arow = iota((64, 128), 0)
    rcol = iota((64, 128), 1)
    same = ((rcol & 3) == (arow >> 4)) & ((rcol >> 4) == ((arow >> 1) & 7))
    want = ((arow & 1) + 1).astype(F32)
    zmask = iota((16, 128), 0) == (iota((16, 128), 1) >> 4)
    dl, dr = iota((128, 128), 0), iota((128, 128), 1)
    extract = jnp.where(dl == ((dr >> 2) & 3) * 32 + ex, 1.0, 0.0).astype(BF16)

    def group(n, carry):
        @pl.when(n < 8)
        def _():
            for p in range(4):
                sy, sx, sends = place(n, p)
                idx = sy * NX + sx

                @pl.when((n > 0) | (p > 0))
                def _():
                    block_copy(0, idx).wait_recv()
                    for way in range(4):
                        @pl.when(sends[way])
                        def _():
                            block_copy(way, idx).start()

            @pl.when(n == 0)
            def _():
                for copy in local[:3]:
                    copy.wait()
                for i in range(3):
                    pltpu.make_async_remote_copy(
                        (wg.at[0], wu.at[0], wd.at[0])[i],
                        (wgu.at[1 - core, :, pl.ds(0, 128)], wgu.at[1 - core, :, pl.ds(128, 128)], wdn.at[1 - core])[i],
                        wssem.at[i], wrsem.at[i], device_id=sibling, device_id_type=MESH).wait_recv()

            for p in range(4):
                sy, sx, _ = place(n, p)
                idx = sy * NX + sx
                got = jnp.dot(tok[idx, 64], extract, preferred_element_type=F32)
                crow = jnp.sum(jnp.where(zmask, got, 0.0), axis=0, keepdims=True)
                sel = jnp.where(same & (crow == want), 1.0, 0.0).astype(BF16)
                raw = jnp.concatenate(
                    [jnp.concatenate([tok[idx, zz * 8 + l] for zz in range(NZ)], axis=0) for l in range(8)], axis=1)
                rows = jnp.dot(sel, raw, preferred_element_type=F32).astype(BF16)
                for q in range(4):
                    xs[p * 16:(p + 1) * 16, q * 1024:(q + 1) * 1024] = rows[q * 16:(q + 1) * 16, :]
            data = xs[...]
            for half in range(2):
                both = jnp.dot(data, wgu[half], preferred_element_type=F32)
                g, u = both[:, :128], both[:, 128:]
                hid[n, z, :, half * 128:(half + 1) * 128] = (g / (1.0 + jnp.exp(-g)) * u).astype(BF16)
            for step in (4, 3, 5, 2, 6, 1, 7):
                hid_copy(n, step).start()

        @pl.when(n >= 1)
        def _():
            b = n - 1
            for step in range(1, NZ):
                src = lax.rem(z + step, NZ)
                pltpu.make_async_remote_copy(
                    hid.at[b, src], hid.at[b, src], hssem.at[b, step], hrsem.at[b, src],
                    device_id=sibling, device_id_type=MESH).wait_recv()
            full = jnp.concatenate([hid[b, zz] for zz in range(NZ)], axis=1)
            for half in range(2):
                cols = jnp.dot(full, wdn[half], preferred_element_type=F32).astype(BF16)
                for p in range(4):
                    outb[b, p, :, half * 256:(half + 1) * 256] = cols[p * 16:(p + 1) * 16]
            for p in range(4):
                if p == 0:
                    @pl.when(b > 0)
                    def _():
                        out_copy(b, 0).start()

                    @pl.when(b == 0)
                    def _():
                        rbuf[ex] = outb[0, 0]
                else:
                    out_copy(b, p).start()

        return carry

    lax.fori_loop(0, 9, group, 0)

    def arrived(step, carry):
        src = lax.rem(ex + step, NE)
        pltpu.make_async_remote_copy(
            outb.at[0, 0], rbuf.at[src], ossem.at[0, 0], orsem.at[src],
            device_id=sibling, device_id_type=MESH).wait_recv()
        return carry

    lax.fori_loop(1, NE, arrived, 0)
    w = wrow[...]
    w_hi = w.astype(BF16)
    w_rest = w - w_hi.astype(F32)
    w_mid = w_rest.astype(BF16)
    w_low = (w_rest - w_mid.astype(F32)).astype(BF16)
    three = jnp.dot(
        jnp.concatenate([w_hi, w_mid, w_low], axis=0), rbuf[...].reshape(NE * 16, 512),
        preferred_element_type=F32)
    total = three[0:32] + three[32:64] + three[64:96]
    for t in range(4):
        for zz in range(NZ):
            fin[zz, t:t + 1, :] = total[t * 8 + zz:t * 8 + zz + 1, :]

    def fin_copy(step):
        peer = lax.rem(z + step, NZ)
        return pltpu.make_async_remote_copy(
            fin.at[peer], final.at[z], fssem.at[step], frsem.at[z],
            device_id=(peer * 2 + core, ex), device_id_type=MESH)

    for step in (4, 3, 5, 2, 6, 1, 7):
        fin_copy(step).start()
    final[z] = fin[z]

    for step in range(1, NZ):
        for copy in z_copy(step):
            copy.wait_send()
    for copy in weights:
        copy.wait_send()

    def drained(n, carry):
        for p in range(4):
            sy, sx, sends = place(n, p)
            idx = sy * NX + sx
            for way in range(4):
                @pl.when(sends[way])
                def _():
                    block_copy(way, idx).wait_send()

            @pl.when((n > 0) | (p > 0))
            def _():
                out_copy(n, p).wait_send()
        for step in range(1, NZ):
            hid_copy(n, step).wait_send()
        return carry

    lax.fori_loop(0, 8, drained, 0)
    for step in range(1, NZ):
        src = lax.rem(z + step, NZ)
        pltpu.make_async_remote_copy(
            fin.at[src], final.at[src], fssem.at[step], frsem.at[src],
            device_id=sibling, device_id_type=MESH).wait_recv()
    for zz in range(NZ):
        out[:, zz * 512:(zz + 1) * 512] = final[zz].astype(BF16)
    for step in range(1, NZ):
        fin_copy(step).wait_send()


def local(tokens, expert_ids, gate_probs, w_gate, w_up, w_down):
    count, width = tokens.shape
    named = (expert_ids[:, :, None] == jnp.arange(NE, dtype=jnp.int32)).astype(F32)
    chosen = jnp.sum(named, axis=1)
    before = [jnp.zeros((NE,), F32)]
    for t in range(1, count):
        before.append(before[-1] + chosen[t - 1])
    code = chosen * (1.0 + jnp.stack(before))
    prob = jnp.sum(named * gate_probs[:, :, None], axis=1)
    meta = jnp.concatenate(
        [code.reshape(1, 128), prob.reshape(1, 128), jnp.zeros((6, 128), F32)], axis=0)
    tiles = tokens.reshape(4, 4, 8, 128).transpose(2, 0, 1, 3).reshape(8, 16, 128)
    vmem = pl.BlockSpec(memory_space=pltpu.VMEM)
    hbm = pl.BlockSpec(memory_space=pl.ANY)
    dma = pltpu.SemaphoreType.DMA
    return pl.pallas_call(
        kernel,
        out_shape=jax.ShapeDtypeStruct((count, width), BF16),
        in_specs=[vmem, vmem, hbm, hbm, hbm],
        out_specs=vmem,
        scratch_shapes=[
            pltpu.VMEM((NE, 65, 16, 128), BF16),
            pltpu.VMEM((NZ, 8, 128), F32),
            pltpu.VMEM((2, 4096, 256), BF16),
            pltpu.VMEM((2, 2048, 256), BF16),
            pltpu.VMEM((64, 4096), BF16),
            pltpu.VMEM((8, NZ, 64, 256), BF16),
            pltpu.VMEM((8, 4, 16, 512), BF16),
            pltpu.VMEM((NE, 16, 512), BF16),
            pltpu.VMEM((32, 512), F32),
            pltpu.VMEM((NZ, 4, 512), F32),
            pltpu.VMEM((NZ, 4, 512), F32),
            dma((5,)), dma((3,)), dma((3,)),
            dma((NZ,)), dma((NZ,)), dma((NZ,)), dma((NZ,)),
            dma((4, NE)), dma((NE,)),
            dma((8, NZ)), dma((8, NZ)),
            dma((8, 4)), dma((NE,)),
            dma((NZ,)), dma((NZ,)),
        ],
        compiler_params=pltpu.CompilerParams(collective_id=0, has_side_effects=True),
    )(tiles, meta, w_gate, w_up, w_down)


def solution(mesh):
    placed = (
        P(("dp", "expert"), None),
        P(("dp", "expert"), None),
        P(("dp", "expert"), None),
        P("expert", None, "dp"),
        P("expert", None, "dp"),
        P("expert", None, "dp"),
    )
    return jax.shard_map(
        local, mesh=mesh, in_specs=placed, out_specs=P(("dp", "expert"), None), check_vma=False
    )
```

```python
import jax
import jax.numpy as jnp
from jax import lax
from jax.experimental import pallas as pl
from jax.experimental.pallas import tpu as pltpu
from jax.sharding import PartitionSpec as P

MESH = pl.DeviceIdType.MESH
NX, NY, NZ = 4, 8, 8
NE = NX * NY
F32, BF16 = jnp.float32, jnp.bfloat16


def iota(shape, dim):
    return lax.broadcasted_iota(jnp.int32, shape, dim)


def kernel(
    tokens, ids, gates, wg, wu, wd, out,
    tok_in, meta_in,
    tok, metaz, wgu, wdn, xs, hid, outb, rbuf, wrow, fin, final,
    lsem, wssem, wrsem, zssem, zrsem, mssem, mrsem, ssem, rsem,
    hssem, hrsem, ossem, orsem, fssem, frsem,
):
    dp = lax.axis_index("dp")
    ex = lax.axis_index("expert")
    z, core = dp // 2, dp % 2
    y, x = ex // NX, ex % NX
    first = core == 0

    local = [
        pltpu.make_async_copy(wg.at[0], wgu.at[core, :, pl.ds(0, 128)], lsem.at[0]),
        pltpu.make_async_copy(wu.at[0], wgu.at[core, :, pl.ds(128, 128)], lsem.at[1]),
        pltpu.make_async_copy(wd.at[0], wdn.at[core], lsem.at[2]),
    ]
    for copy in local:
        copy.start()

    barrier = pltpu.get_barrier_semaphore()

    def greet(step, carry):
        peer = lax.rem(ex + step, NE)
        pl.semaphore_signal(barrier, inc=1, device_id=(dp, peer), device_id_type=MESH)
        return carry

    lax.fori_loop(1, NE, greet, 0)
    for step in range(1, NZ):
        peer = lax.rem(z + step, NZ) * 2 + core
        pl.semaphore_signal(barrier, inc=1, device_id=(peer, ex), device_id_type=MESH)
    pl.semaphore_signal(barrier, inc=1, device_id=(z * 2 + 1 - core, ex), device_id_type=MESH)

    at = iota((8, 128), 1)
    chosen, prob = jnp.zeros((8, 128), F32), jnp.zeros((8, 128), F32)
    for t in range(4):
        for k in range(8):
            hit = at == ids[t:t + 1, k:k + 1] + t * 32
            chosen = jnp.where(hit, 1.0, chosen)
            prob = jnp.where(hit, gates[t:t + 1, k:k + 1], prob)
    before = jnp.zeros((8, 128), F32)
    for t in range(1, 4):
        before = before + jnp.where(at >= 32 * t, pltpu.roll(chosen, 32 * t, 1), 0.0)
    meta_in[...] = jnp.where(iota((8, 128), 0) == 0, chosen * (1.0 + before), prob)
    metaz[z] = meta_in[...]
    wide_tokens = tokens[...].astype(F32)
    for l in range(8):
        tile = jnp.concatenate(
            [wide_tokens[:, q * 1024 + l * 128:q * 1024 + (l + 1) * 128] for q in range(4)], axis=0).astype(BF16)
        tok_in[l] = tile
        tok[ex, 8 + l] = tile
    pl.semaphore_wait(barrier, NE - 1 + NZ - 1 + 1)

    def z_copy(step):
        peer = lax.rem(z + step, NZ)
        return (
            pltpu.make_async_remote_copy(
                meta_in, metaz.at[z], mssem.at[step], mrsem.at[z],
                device_id=(peer * 2 + core, ex), device_id_type=MESH),
            pltpu.make_async_remote_copy(
                tok_in, tok.at[ex, pl.ds((9 - step) % NZ * 8, 8)], zssem.at[step], zrsem.at[NZ - step],
                device_id=(peer * 2 + core, ex), device_id_type=MESH),
        )

    for step in (7, 1, 6, 5, 2, 4, 3):
        for copy in z_copy(step)[::-1]:
            copy.start()

    def z_arrived(step):
        pltpu.make_async_remote_copy(
            tok_in, tok.at[ex, pl.ds((step + 1) % NZ * 8, 8)], zssem.at[step], zrsem.at[step],
            device_id=sibling, device_id_type=MESH).wait_recv()

    sibling = (z * 2 + 1 - core, ex)
    weights = [
        pltpu.make_async_remote_copy(
            wg.at[0], wgu.at[core, :, pl.ds(0, 128)], wssem.at[0], wrsem.at[0],
            device_id=sibling, device_id_type=MESH),
        pltpu.make_async_remote_copy(
            wu.at[0], wgu.at[core, :, pl.ds(128, 128)], wssem.at[1], wrsem.at[1],
            device_id=sibling, device_id_type=MESH),
        pltpu.make_async_remote_copy(
            wd.at[0], wdn.at[core], wssem.at[2], wrsem.at[2],
            device_id=sibling, device_id_type=MESH),
    ]
    for copy in weights:
        copy.start()

    def place(n, p):
        m = n - 1
        k = m // 2 + 1
        h = m % 2
        i0 = jnp.where(n == 0, p, jnp.where(n == 7, p, 2 * h + p // 2))
        dx0 = jnp.where(i0 == 0, 0, jnp.where(i0 == 1, -1, i0 - 1))
        dy0 = jnp.where(n == 0, 0, jnp.where(n == 7, -4, -k if p % 2 == 0 else k))
        own = (n == 0) | (n == 2)
        opp = n >= 6
        mm = jnp.where(n == 1, 0, n - 2)
        j = jnp.where(own, 2 * n + p, jnp.where(opp, (n - 6) * 4 + p, 2 * mm + p // 2))
        half = (j + 1) // 2
        dy1 = jnp.where(j % 2 == 1, -half, half)
        dx1 = jnp.where(own, 0, jnp.where(opp, 2, -1 if p % 2 == 0 else 1))
        dx = jnp.where(first, dx0, dx1)
        dy = jnp.where(first, dy0, dy1)
        sx = lax.rem(x + dx + NX, NX)
        sy = lax.rem(y + dy + NY, NY)
        mid = (n >= 1) & (n <= 6)
        upto = (k <= 2) | ((k == 3) & (h == (0 if p % 2 == 0 else 1)))
        row = n == 0
        xp0 = row & (p <= 1)
        xm0 = row & (p == 0)
        yp0 = row | (mid & upto & (p % 2 == 0))
        ym0 = row | (mid & upto & (p % 2 == 1))
        side = ~own & ~opp
        xp1 = own | (side & (p == 0))
        xm1 = own | (side & (p == 3))
        yp1 = own & ((j == 0) | ((j % 2 == 1) & (j <= 5)))
        ym1 = own & ((j == 0) | ((j % 2 == 0) & (j >= 2) & (j <= 4)))

        def pick(a, b):
            return (first & a) | (~first & b)

        sends = (pick(xp0, xp1), pick(xm0, xm1), pick(yp0, yp1), pick(ym0, ym1))
        return sy, sx, sends

    right, left = lax.rem(x + 1, NX), lax.rem(x + NX - 1, NX)
    below, above = lax.rem(y + 1, NY), lax.rem(y + NY - 1, NY)
    targets = ((dp, y * NX + right), (dp, y * NX + left), (dp, below * NX + x), (dp, above * NX + x))

    def block_copy(way, idx, part):
        piece = tok.at[idx, pl.ds(0, 32)] if part == 0 else tok.at[idx, pl.ds(32, 33)]
        return pltpu.make_async_remote_copy(
            piece, piece, ssem.at[part, way, idx], rsem.at[part, idx],
            device_id=targets[way], device_id_type=MESH)

    def hid_copy(n, step):
        peer = lax.rem(z + step, NZ)
        return pltpu.make_async_remote_copy(
            hid.at[n, z], hid.at[n, z], hssem.at[n, step], hrsem.at[n, z],
            device_id=(peer * 2 + core, ex), device_id_type=MESH)

    def out_copy(n, p):
        sy, sx, _ = place(n, p)
        return pltpu.make_async_remote_copy(
            outb.at[n, p], rbuf.at[ex], ossem.at[n, p], orsem.at[ex],
            device_id=(dp, sy * NX + sx), device_id_type=MESH)

    order = (2, 3, 0, 1)
    for step in (7, 1, 2):
        z_arrived(step)
    for way in order:
        block_copy(way, ex, 0).start()
    for step in range(1, NZ):
        src = lax.rem(z + step, NZ)
        pltpu.make_async_remote_copy(
            meta_in, metaz.at[src], mssem.at[step], mrsem.at[src],
            device_id=sibling, device_id_type=MESH).wait_recv()
    codes = metaz[:, 0, :]
    tok[ex, 64] = jnp.concatenate([codes, jnp.zeros_like(codes)], axis=0).astype(BF16)
    for step in (6, 5, 3, 4):
        z_arrived(step)
    for way in order:
        block_copy(way, ex, 1).start()

    lane = iota((8, 512), 1)
    sub = iota((8, 512), 0)
    depth = iota((128, 512), 0)
    wide = iota((128, 512), 1)
    probs = metaz[:, 1, :]
    hi = probs.astype(BF16)
    rest = probs - hi.astype(F32)
    mid_part = rest.astype(BF16)
    low = (rest - mid_part.astype(F32)).astype(BF16)
    stack = jnp.concatenate([codes.astype(BF16), hi, mid_part, low], axis=0)
    for t in range(4):
        spread = jnp.where(depth == t * 32 + (wide >> 4), 1.0, 0.0).astype(BF16)
        got = jnp.dot(stack, spread, preferred_element_type=F32)
        code = got[0:8]
        prob = got[8:16] + got[16:24] + got[24:32]
        keep = (((lane >> 1) & 7) == sub) & (code == ((lane & 1) + 1).astype(F32))
        wrow[t * 8:(t + 1) * 8, :] = jnp.where(keep, prob, 0.0)

    arow = iota((64, 128), 0)
    rcol = iota((64, 128), 1)
    from_z = ((rcol >> 4) + z + 7) & 7
    same = (((rcol >> 2) & 3) == (arow >> 4)) & (from_z == ((arow >> 1) & 7))
    want = ((arow & 1) + 1).astype(F32)
    zmask = iota((16, 128), 0) == (((iota((16, 128), 1) >> 4) + z + 7) & 7)
    dl, dr = iota((128, 128), 0), iota((128, 128), 1)
    extract = jnp.where(dl == (dr & 3) * 32 + ex, 1.0, 0.0).astype(BF16)

    def group(n, carry):
        @pl.when(n < 8)
        def _():
            for p in range(4):
                sy, sx, sends = place(n, p)
                idx = sy * NX + sx

                @pl.when((n > 0) | (p > 0))
                def _():
                    for part in range(2):
                        block_copy(0, idx, part).wait_recv()
                        for way in range(4):
                            @pl.when(sends[way])
                            def _():
                                block_copy(way, idx, part).start()

            @pl.when(n == 0)
            def _():
                for copy in local:
                    copy.wait()
                for i in range(3):
                    pltpu.make_async_remote_copy(
                        (wg.at[0], wu.at[0], wd.at[0])[i],
                        (wgu.at[1 - core, :, pl.ds(0, 128)], wgu.at[1 - core, :, pl.ds(128, 128)], wdn.at[1 - core])[i],
                        wssem.at[i], wrsem.at[i], device_id=sibling, device_id_type=MESH).wait_recv()

            for p in range(4):
                sy, sx, _ = place(n, p)
                idx = sy * NX + sx
                got = jnp.dot(tok[idx, 64], extract, preferred_element_type=F32)
                crow = jnp.sum(jnp.where(zmask, got, 0.0), axis=0, keepdims=True)
                sel = jnp.where(same & (crow == want), 1.0, 0.0).astype(BF16)
                raw = jnp.concatenate(
                    [jnp.concatenate([tok[idx, zz * 8 + l] for zz in range(NZ)], axis=0) for l in range(8)], axis=1)
                rows = jnp.dot(sel, raw, preferred_element_type=F32).astype(BF16)
                for q in range(4):
                    xs[p * 16:(p + 1) * 16, q * 1024:(q + 1) * 1024] = rows[q * 16:(q + 1) * 16, :]
            data = xs[...]
            for half in range(2):
                both = jnp.dot(data, wgu[half], preferred_element_type=F32)
                g, u = both[:, :128], both[:, 128:]
                hid[n, z, :, half * 128:(half + 1) * 128] = (g / (1.0 + jnp.exp(-g)) * u).astype(BF16)
            for step in (4, 3, 5, 2, 6, 1, 7):
                hid_copy(n, step).start()

        @pl.when(n >= 1)
        def _():
            b = n - 1
            for step in range(1, NZ):
                src = lax.rem(z + step, NZ)
                pltpu.make_async_remote_copy(
                    hid.at[b, src], hid.at[b, src], hssem.at[b, step], hrsem.at[b, src],
                    device_id=sibling, device_id_type=MESH).wait_recv()
            full = jnp.concatenate([hid[b, zz] for zz in range(NZ)], axis=1)
            for half in range(2):
                cols = jnp.dot(full, wdn[half], preferred_element_type=F32).astype(BF16)
                for p in range(4):
                    outb[b, p, :, half * 256:(half + 1) * 256] = cols[p * 16:(p + 1) * 16]
            for p in range(4):
                if p == 0:
                    @pl.when(b > 0)
                    def _():
                        out_copy(b, 0).start()

                    @pl.when(b == 0)
                    def _():
                        rbuf[ex] = outb[0, 0]
                else:
                    out_copy(b, p).start()

        return carry

    lax.fori_loop(0, 9, group, 0)

    def arrived(step, carry):
        src = lax.rem(ex + step, NE)
        pltpu.make_async_remote_copy(
            outb.at[0, 0], rbuf.at[src], ossem.at[0, 0], orsem.at[src],
            device_id=sibling, device_id_type=MESH).wait_recv()
        return carry

    lax.fori_loop(1, NE, arrived, 0)
    w = wrow[...]
    w_hi = w.astype(BF16)
    w_rest = w - w_hi.astype(F32)
    w_mid = w_rest.astype(BF16)
    w_low = (w_rest - w_mid.astype(F32)).astype(BF16)
    three = jnp.dot(
        jnp.concatenate([w_hi, w_mid, w_low], axis=0), rbuf[...].reshape(NE * 16, 512),
        preferred_element_type=F32)
    total = three[0:32] + three[32:64] + three[64:96]
    for t in range(4):
        for zz in range(NZ):
            fin[zz, t:t + 1, :] = total[t * 8 + zz:t * 8 + zz + 1, :]

    def fin_copy(step):
        peer = lax.rem(z + step, NZ)
        return pltpu.make_async_remote_copy(
            fin.at[peer], final.at[z], fssem.at[step], frsem.at[z],
            device_id=(peer * 2 + core, ex), device_id_type=MESH)

    for step in (4, 3, 5, 2, 6, 1, 7):
        fin_copy(step).start()
    final[z] = fin[z]

    for step in range(1, NZ):
        for copy in z_copy(step):
            copy.wait_send()
    for copy in weights:
        copy.wait_send()

    def drained(n, carry):
        for p in range(4):
            sy, sx, sends = place(n, p)
            idx = sy * NX + sx
            for way in range(4):
                @pl.when(sends[way])
                def _():
                    block_copy(way, idx, 0).wait_send()
                    block_copy(way, idx, 1).wait_send()

            @pl.when((n > 0) | (p > 0))
            def _():
                out_copy(n, p).wait_send()
        for step in range(1, NZ):
            hid_copy(n, step).wait_send()
        return carry

    lax.fori_loop(0, 8, drained, 0)
    for step in range(1, NZ):
        src = lax.rem(z + step, NZ)
        pltpu.make_async_remote_copy(
            fin.at[src], final.at[src], fssem.at[step], frsem.at[src],
            device_id=sibling, device_id_type=MESH).wait_recv()
    for zz in range(NZ):
        out[:, zz * 512:(zz + 1) * 512] = final[zz].astype(BF16)
    for step in range(1, NZ):
        fin_copy(step).wait_send()


def local(tokens, expert_ids, gate_probs, w_gate, w_up, w_down):
    count, width = tokens.shape
    vmem = pl.BlockSpec(memory_space=pltpu.VMEM)
    hbm = pl.BlockSpec(memory_space=pl.ANY)
    dma = pltpu.SemaphoreType.DMA
    return pl.pallas_call(
        kernel,
        out_shape=jax.ShapeDtypeStruct((count, width), BF16),
        in_specs=[vmem, vmem, vmem, hbm, hbm, hbm],
        out_specs=vmem,
        scratch_shapes=[
            pltpu.VMEM((8, 16, 128), BF16),
            pltpu.VMEM((8, 128), F32),
            pltpu.VMEM((NE, 65, 16, 128), BF16),
            pltpu.VMEM((NZ, 8, 128), F32),
            pltpu.VMEM((2, 4096, 256), BF16),
            pltpu.VMEM((2, 2048, 256), BF16),
            pltpu.VMEM((64, 4096), BF16),
            pltpu.VMEM((8, NZ, 64, 256), BF16),
            pltpu.VMEM((8, 4, 16, 512), BF16),
            pltpu.VMEM((NE, 16, 512), BF16),
            pltpu.VMEM((32, 512), F32),
            pltpu.VMEM((NZ, 4, 512), F32),
            pltpu.VMEM((NZ, 4, 512), F32),
            dma((3,)), dma((3,)), dma((3,)),
            dma((NZ,)), dma((NZ,)), dma((NZ,)), dma((NZ,)),
            dma((2, 4, NE)), dma((2, NE)),
            dma((8, NZ)), dma((8, NZ)),
            dma((8, 4)), dma((NE,)),
            dma((NZ,)), dma((NZ,)),
        ],
        compiler_params=pltpu.CompilerParams(collective_id=0, has_side_effects=True),
    )(tokens, expert_ids, gate_probs, w_gate, w_up, w_down)


def solution(mesh):
    placed = (
        P(("dp", "expert"), None),
        P(("dp", "expert"), None),
        P(("dp", "expert"), None),
        P("expert", None, "dp"),
        P("expert", None, "dp"),
        P("expert", None, "dp"),
    )
    return jax.shard_map(
        local, mesh=mesh, in_specs=placed, out_specs=P(("dp", "expert"), None), check_vma=False
    )
```

```python
import jax
import jax.numpy as jnp
from jax import lax
from jax.experimental import pallas as pl
from jax.experimental.pallas import tpu as pltpu
from jax.sharding import PartitionSpec as P

MESH = pl.DeviceIdType.MESH
NX, NY, NZ = 4, 8, 8
NE = NX * NY
F32, BF16 = jnp.float32, jnp.bfloat16


def iota(shape, dim):
    return lax.broadcasted_iota(jnp.int32, shape, dim)


def kernel(
    tokens, ids, gates, wg, wu, wd, out,
    tok_in, meta_in,
    tok, metaz, wgu, wdn, xs, hid, outb, rbuf, wrow, fin, final,
    lsem, wssem, wrsem, zssem, zrsem, mssem, mrsem, ssem, rsem,
    hssem, hrsem, ossem, orsem, fssem, frsem,
):
    dp = lax.axis_index("dp")
    ex = lax.axis_index("expert")
    z, core = dp // 2, dp % 2
    y, x = ex // NX, ex % NX
    first = core == 0

    local = [
        pltpu.make_async_copy(wg.at[0], wgu.at[core, :, pl.ds(0, 128)], lsem.at[0]),
        pltpu.make_async_copy(wu.at[0], wgu.at[core, :, pl.ds(128, 128)], lsem.at[1]),
        pltpu.make_async_copy(wd.at[0], wdn.at[core], lsem.at[2]),
    ]
    for copy in local:
        copy.start()

    barrier = pltpu.get_barrier_semaphore()

    def greet(step, carry):
        peer = lax.rem(ex + step, NE)
        pl.semaphore_signal(barrier, inc=1, device_id=(dp, peer), device_id_type=MESH)
        return carry

    lax.fori_loop(1, NE, greet, 0)
    for step in range(1, NZ):
        peer = lax.rem(z + step, NZ) * 2 + core
        pl.semaphore_signal(barrier, inc=1, device_id=(peer, ex), device_id_type=MESH)
    pl.semaphore_signal(barrier, inc=1, device_id=(z * 2 + 1 - core, ex), device_id_type=MESH)

    at = iota((8, 128), 1)
    chosen, prob = jnp.zeros((8, 128), F32), jnp.zeros((8, 128), F32)
    for t in range(4):
        for k in range(8):
            hit = at == ids[t:t + 1, k:k + 1] + t * 32
            chosen = jnp.where(hit, 1.0, chosen)
            prob = jnp.where(hit, gates[t:t + 1, k:k + 1], prob)
    before = jnp.zeros((8, 128), F32)
    for t in range(1, 4):
        before = before + jnp.where(at >= 32 * t, pltpu.roll(chosen, 32 * t, 1), 0.0)
    meta_in[...] = jnp.where(iota((8, 128), 0) == 0, chosen * (1.0 + before), prob)
    metaz[z] = meta_in[...]
    wide_tokens = tokens[...].astype(F32)
    for l in range(8):
        tile = jnp.concatenate(
            [wide_tokens[:, q * 1024 + l * 128:q * 1024 + (l + 1) * 128] for q in range(4)], axis=0).astype(BF16)
        tok_in[l] = tile
        tok[ex, 8 + l] = tile
    pl.semaphore_wait(barrier, NE - 1 + NZ - 1 + 1)

    def z_copy(step):
        peer = lax.rem(z + step, NZ)
        return (
            pltpu.make_async_remote_copy(
                meta_in, metaz.at[z], mssem.at[step], mrsem.at[z],
                device_id=(peer * 2 + core, ex), device_id_type=MESH),
            pltpu.make_async_remote_copy(
                tok_in, tok.at[ex, pl.ds((9 - step) % NZ * 8, 8)], zssem.at[step], zrsem.at[NZ - step],
                device_id=(peer * 2 + core, ex), device_id_type=MESH),
        )

    for step in (7, 1, 6, 5, 2, 4, 3):
        for copy in z_copy(step)[::-1]:
            copy.start()

    def z_arrived(step):
        pltpu.make_async_remote_copy(
            tok_in, tok.at[ex, pl.ds((step + 1) % NZ * 8, 8)], zssem.at[step], zrsem.at[step],
            device_id=sibling, device_id_type=MESH).wait_recv()

    sibling = (z * 2 + 1 - core, ex)
    weights = [
        pltpu.make_async_remote_copy(
            wg.at[0], wgu.at[core, :, pl.ds(0, 128)], wssem.at[0], wrsem.at[0],
            device_id=sibling, device_id_type=MESH),
        pltpu.make_async_remote_copy(
            wu.at[0], wgu.at[core, :, pl.ds(128, 128)], wssem.at[1], wrsem.at[1],
            device_id=sibling, device_id_type=MESH),
        pltpu.make_async_remote_copy(
            wd.at[0], wdn.at[core], wssem.at[2], wrsem.at[2],
            device_id=sibling, device_id_type=MESH),
    ]
    for copy in weights:
        copy.start()

    def place(n, p):
        m = n - 1
        k = m // 2 + 1
        h = m % 2
        i0 = jnp.where(n == 0, p, jnp.where(n == 7, p, 2 * h + p // 2))
        dx0 = jnp.where(i0 == 0, 0, jnp.where(i0 == 1, -1, i0 - 1))
        dy0 = jnp.where(n == 0, 0, jnp.where(n == 7, -4, -k if p % 2 == 0 else k))
        own = (n == 0) | (n == 2)
        opp = n >= 6
        mm = jnp.where(n == 1, 0, n - 2)
        j = jnp.where(own, 2 * n + p, jnp.where(opp, (n - 6) * 4 + p, 2 * mm + p // 2))
        half = (j + 1) // 2
        dy1 = jnp.where(j % 2 == 1, -half, half)
        dx1 = jnp.where(own, 0, jnp.where(opp, 2, -1 if p % 2 == 0 else 1))
        dx = jnp.where(first, dx0, dx1)
        dy = jnp.where(first, dy0, dy1)
        sx = lax.rem(x + dx + NX, NX)
        sy = lax.rem(y + dy + NY, NY)
        mid = (n >= 1) & (n <= 6)
        upto = (k <= 2) | ((k == 3) & (h == (0 if p % 2 == 0 else 1)))
        row = n == 0
        xp0 = row & (p <= 1)
        xm0 = row & (p == 0)
        yp0 = row | (mid & upto & (p % 2 == 0))
        ym0 = row | (mid & upto & (p % 2 == 1))
        side = ~own & ~opp
        xp1 = own | (side & (p == 0))
        xm1 = own | (side & (p == 3))
        yp1 = own & ((j == 0) | ((j % 2 == 1) & (j <= 5)))
        ym1 = own & ((j == 0) | ((j % 2 == 0) & (j >= 2) & (j <= 4)))

        def pick(a, b):
            return (first & a) | (~first & b)

        sends = (pick(xp0, xp1), pick(xm0, xm1), pick(yp0, yp1), pick(ym0, ym1))
        return sy, sx, sends

    right, left = lax.rem(x + 1, NX), lax.rem(x + NX - 1, NX)
    below, above = lax.rem(y + 1, NY), lax.rem(y + NY - 1, NY)
    targets = ((dp, y * NX + right), (dp, y * NX + left), (dp, below * NX + x), (dp, above * NX + x))

    def block_copy(way, idx, part):
        piece = tok.at[idx, pl.ds(0, 32)] if part == 0 else tok.at[idx, pl.ds(32, 33)]
        return pltpu.make_async_remote_copy(
            piece, piece, ssem.at[part, way, idx], rsem.at[part, idx],
            device_id=targets[way], device_id_type=MESH)

    def hid_copy(n, step):
        peer = lax.rem(z + step, NZ)
        return pltpu.make_async_remote_copy(
            hid.at[n, z], hid.at[n, z], hssem.at[n, step], hrsem.at[n, z],
            device_id=(peer * 2 + core, ex), device_id_type=MESH)

    def out_copy(n, p):
        sy, sx, _ = place(n, p)
        return pltpu.make_async_remote_copy(
            outb.at[n, p], rbuf.at[ex], ossem.at[n, p], orsem.at[ex],
            device_id=(dp, sy * NX + sx), device_id_type=MESH)

    order = (2, 3, 0, 1)
    for step in (7, 1, 2):
        z_arrived(step)
    for way in order:
        block_copy(way, ex, 0).start()
    for step in range(1, NZ):
        src = lax.rem(z + step, NZ)
        pltpu.make_async_remote_copy(
            meta_in, metaz.at[src], mssem.at[step], mrsem.at[src],
            device_id=sibling, device_id_type=MESH).wait_recv()
    codes = metaz[:, 0, :]
    tok[ex, 64] = jnp.concatenate([codes, jnp.zeros_like(codes)], axis=0).astype(BF16)
    for step in (6, 5, 3, 4):
        z_arrived(step)
    for way in order:
        block_copy(way, ex, 1).start()

    lane = iota((8, 512), 1)
    sub = iota((8, 512), 0)
    depth = iota((128, 512), 0)
    wide = iota((128, 512), 1)
    probs = metaz[:, 1, :]
    hi = probs.astype(BF16)
    rest = probs - hi.astype(F32)
    mid_part = rest.astype(BF16)
    low = (rest - mid_part.astype(F32)).astype(BF16)
    stack = jnp.concatenate([codes.astype(BF16), hi, mid_part, low], axis=0)
    for t in range(4):
        spread = jnp.where(depth == t * 32 + (wide >> 4), 1.0, 0.0).astype(BF16)
        got = jnp.dot(stack, spread, preferred_element_type=F32)
        code = got[0:8]
        prob = got[8:16] + got[16:24] + got[24:32]
        keep = (((lane >> 1) & 7) == sub) & (code == ((lane & 1) + 1).astype(F32))
        wrow[t * 8:(t + 1) * 8, :] = jnp.where(keep, prob, 0.0)

    arow = iota((64, 128), 0)
    rcol = iota((64, 128), 1)
    from_z = ((rcol >> 4) + z + 7) & 7
    same = (((rcol >> 2) & 3) == (arow >> 4)) & (from_z == ((arow >> 1) & 7))
    want = ((arow & 1) + 1).astype(F32)
    zmask = iota((16, 128), 0) == (((iota((16, 128), 1) >> 4) + z + 7) & 7)
    dl, dr = iota((128, 128), 0), iota((128, 128), 1)
    extract = jnp.where(dl == (dr & 3) * 32 + ex, 1.0, 0.0).astype(BF16)

    def group(n, carry):
        @pl.when(n < 8)
        def _():
            for p in range(4):
                sy, sx, sends = place(n, p)
                idx = sy * NX + sx

                @pl.when((n > 0) | (p > 0))
                def _():
                    for part in range(2):
                        block_copy(0, idx, part).wait_recv()
                        for way in range(4):
                            @pl.when(sends[way])
                            def _():
                                block_copy(way, idx, part).start()

            @pl.when(n == 0)
            def _():
                for copy in local:
                    copy.wait()
                for i in range(3):
                    pltpu.make_async_remote_copy(
                        (wg.at[0], wu.at[0], wd.at[0])[i],
                        (wgu.at[1 - core, :, pl.ds(0, 128)], wgu.at[1 - core, :, pl.ds(128, 128)], wdn.at[1 - core])[i],
                        wssem.at[i], wrsem.at[i], device_id=sibling, device_id_type=MESH).wait_recv()

            for p in range(4):
                sy, sx, _ = place(n, p)
                idx = sy * NX + sx
                got = jnp.dot(tok[idx, 64], extract, preferred_element_type=F32)
                crow = jnp.sum(jnp.where(zmask, got, 0.0), axis=0, keepdims=True)
                sel = jnp.where(same & (crow == want), 1.0, 0.0).astype(BF16)
                raw = jnp.concatenate(
                    [jnp.concatenate([tok[idx, zz * 8 + l] for zz in range(NZ)], axis=0) for l in range(8)], axis=1)
                rows = jnp.dot(sel, raw, preferred_element_type=F32).astype(BF16)
                for q in range(4):
                    xs[p * 16:(p + 1) * 16, q * 1024:(q + 1) * 1024] = rows[q * 16:(q + 1) * 16, :]
            data = xs[...]
            for half in range(2):
                both = jnp.dot(data, wgu[half], preferred_element_type=F32)
                g, u = both[:, :128], both[:, 128:]
                hid[n, z, :, half * 128:(half + 1) * 128] = (g / (1.0 + jnp.exp(-g)) * u).astype(BF16)
            for step in (4, 3, 5, 2, 6, 1, 7):
                hid_copy(n, step).start()

        @pl.when(n >= 3)
        def _():
            b = n - 3
            for step in range(1, NZ):
                src = lax.rem(z + step, NZ)
                pltpu.make_async_remote_copy(
                    hid.at[b, src], hid.at[b, src], hssem.at[b, step], hrsem.at[b, src],
                    device_id=sibling, device_id_type=MESH).wait_recv()
            full = jnp.concatenate([hid[b, zz] for zz in range(NZ)], axis=1)
            for half in range(2):
                cols = jnp.dot(full, wdn[half], preferred_element_type=F32).astype(BF16)
                for p in range(4):
                    outb[b, p, :, half * 256:(half + 1) * 256] = cols[p * 16:(p + 1) * 16]
            for p in range(4):
                if p == 0:
                    @pl.when(b > 0)
                    def _():
                        out_copy(b, 0).start()

                    @pl.when(b == 0)
                    def _():
                        rbuf[ex] = outb[0, 0]
                else:
                    out_copy(b, p).start()

        return carry

    lax.fori_loop(0, 11, group, 0)

    def arrived(step, carry):
        src = lax.rem(ex + step, NE)
        pltpu.make_async_remote_copy(
            outb.at[0, 0], rbuf.at[src], ossem.at[0, 0], orsem.at[src],
            device_id=sibling, device_id_type=MESH).wait_recv()
        return carry

    lax.fori_loop(1, NE, arrived, 0)
    w = wrow[...]
    w_hi = w.astype(BF16)
    w_rest = w - w_hi.astype(F32)
    w_mid = w_rest.astype(BF16)
    w_low = (w_rest - w_mid.astype(F32)).astype(BF16)
    three = jnp.dot(
        jnp.concatenate([w_hi, w_mid, w_low], axis=0), rbuf[...].reshape(NE * 16, 512),
        preferred_element_type=F32)
    total = three[0:32] + three[32:64] + three[64:96]
    for t in range(4):
        for zz in range(NZ):
            fin[zz, t:t + 1, :] = total[t * 8 + zz:t * 8 + zz + 1, :]

    def fin_copy(step):
        peer = lax.rem(z + step, NZ)
        return pltpu.make_async_remote_copy(
            fin.at[peer], final.at[z], fssem.at[step], frsem.at[z],
            device_id=(peer * 2 + core, ex), device_id_type=MESH)

    for step in (4, 3, 5, 2, 6, 1, 7):
        fin_copy(step).start()
    final[z] = fin[z]

    for step in range(1, NZ):
        for copy in z_copy(step):
            copy.wait_send()
    for copy in weights:
        copy.wait_send()

    def drained(n, carry):
        for p in range(4):
            sy, sx, sends = place(n, p)
            idx = sy * NX + sx
            for way in range(4):
                @pl.when(sends[way])
                def _():
                    block_copy(way, idx, 0).wait_send()
                    block_copy(way, idx, 1).wait_send()

            @pl.when((n > 0) | (p > 0))
            def _():
                out_copy(n, p).wait_send()
        for step in range(1, NZ):
            hid_copy(n, step).wait_send()
        return carry

    lax.fori_loop(0, 8, drained, 0)
    for step in range(1, NZ):
        src = lax.rem(z + step, NZ)
        pltpu.make_async_remote_copy(
            fin.at[src], final.at[src], fssem.at[step], frsem.at[src],
            device_id=sibling, device_id_type=MESH).wait_recv()
    for zz in range(NZ):
        out[:, zz * 512:(zz + 1) * 512] = final[zz].astype(BF16)
    for step in range(1, NZ):
        fin_copy(step).wait_send()


def local(tokens, expert_ids, gate_probs, w_gate, w_up, w_down):
    count, width = tokens.shape
    vmem = pl.BlockSpec(memory_space=pltpu.VMEM)
    hbm = pl.BlockSpec(memory_space=pl.ANY)
    dma = pltpu.SemaphoreType.DMA
    return pl.pallas_call(
        kernel,
        out_shape=jax.ShapeDtypeStruct((count, width), BF16),
        in_specs=[vmem, vmem, vmem, hbm, hbm, hbm],
        out_specs=vmem,
        scratch_shapes=[
            pltpu.VMEM((8, 16, 128), BF16),
            pltpu.VMEM((8, 128), F32),
            pltpu.VMEM((NE, 65, 16, 128), BF16),
            pltpu.VMEM((NZ, 8, 128), F32),
            pltpu.VMEM((2, 4096, 256), BF16),
            pltpu.VMEM((2, 2048, 256), BF16),
            pltpu.VMEM((64, 4096), BF16),
            pltpu.VMEM((8, NZ, 64, 256), BF16),
            pltpu.VMEM((8, 4, 16, 512), BF16),
            pltpu.VMEM((NE, 16, 512), BF16),
            pltpu.VMEM((32, 512), F32),
            pltpu.VMEM((NZ, 4, 512), F32),
            pltpu.VMEM((NZ, 4, 512), F32),
            dma((3,)), dma((3,)), dma((3,)),
            dma((NZ,)), dma((NZ,)), dma((NZ,)), dma((NZ,)),
            dma((2, 4, NE)), dma((2, NE)),
            dma((8, NZ)), dma((8, NZ)),
            dma((8, 4)), dma((NE,)),
            dma((NZ,)), dma((NZ,)),
        ],
        compiler_params=pltpu.CompilerParams(collective_id=0, has_side_effects=True),
    )(tokens, expert_ids, gate_probs, w_gate, w_up, w_down)


def solution(mesh):
    placed = (
        P(("dp", "expert"), None),
        P(("dp", "expert"), None),
        P(("dp", "expert"), None),
        P("expert", None, "dp"),
        P("expert", None, "dp"),
        P("expert", None, "dp"),
    )
    return jax.shard_map(
        local, mesh=mesh, in_specs=placed, out_specs=P(("dp", "expert"), None), check_vma=False
    )
```
